512 devices in a mesh: chol: 8 (over x, y_hi), walk: 64 (over z, y_lo, core).
Axes of the slice: x: 4, y: 4 (y_hi: 2, y_lo: 2; y = y_hi * 2 + y_lo), z: 16, core: 2. Of those that a mesh axis runs over, the one named last changes fastest.
Arguments:
- field_draws: bfloat16 [64, 2048], P('walk', 'chol'), may hold values from -6 to 6
- chol_vectors: bfloat16 [2048, 512, 512], P('chol', 'walk'), as said below
- rotated_vectors: bfloat16 [2048, 128, 512], P(('chol', 'walk')), may hold values from -1.5 to 1.5
- walkers: bfloat16 [64, 512, 128], P('walk'), may hold values from -6 to 6
Outputs:
- propagated: float32 [64, 512, 128], P('walk')
- exchange_energy: float32 [64], P('walk')
The draws below stay inside these ranges and needn't reach their ends.
Inputs may be any that keep to these rules, and one draw needn't show every extreme that they name: Each chol_vectors[g] is a symmetric matrix.
All inputs are finite; a program needn't handle non-finite values.
Results may differ from the reference program's by a relative error of at most 0.0036.
Values may be sent and summed in bfloat16 or wider, within the bound.
A program may use at most 64 MiB of HBM per device.

```python
from functools import partial
import jax
import jax.numpy as jnp
from jax import lax

ORB = 512
OCC = 128
VECS = 2048
TERMS = 4
WALKERS = 64


def draw_chol_vectors(key, part):
    scale = 1.1 / (VECS * ORB) ** 0.5
    raw = jax.random.truncated_normal(key, -6.0, 6.0, (VECS, ORB, ORB), jnp.float32)
    sym = (raw + jnp.swapaxes(raw, 1, 2)) * (scale / 2.0 ** 0.5)
    return sym.astype(jnp.bfloat16)


def steps_of(own_key, shape, pieces, least, largest):
    loudness, own = 1.0, jax.random.fold_in(own_key, 6)
    for position, shards_of in pieces:
        draws = jnp.exp(jax.random.uniform(jax.random.fold_in(own, position), (shards_of,), jnp.float32, least / len(pieces), largest / len(pieces)))
        loudness = loudness * jnp.repeat(draws, shape[position] // shards_of).reshape([-1 if axis == position else 1 for axis in range(len(shape))])
    return loudness


def centred(own_key, extent, scale, limit, pieces=(), dtype=jnp.bfloat16):
    entries = scale * jax.random.normal(own_key, extent, jnp.float32)
    if pieces:
        entries = entries * steps_of(own_key, extent, pieces, -0.22, 0.18)
    return jnp.clip(entries, -limit, limit).astype(dtype)


def setup_inputs(seed: int = 0) -> dict:
    key_list = jax.random.split(jax.random.key(seed), 5)
    field_draws = centred(key_list[0], (WALKERS, VECS), 1.0, 6.0, ((0, 64), (1, 8)))
    chol_vectors = draw_chol_vectors(jax.random.fold_in(key_list[4], 71), 0)
    rotated_vectors = centred(key_list[2], (VECS, OCC, ORB), ((6 * ORB / (VECS * OCC)) ** 0.5), 1.5, ((0, 512),))
    walkers = centred(key_list[3], (WALKERS, ORB, OCC), 1.0, 6.0, ((0, 64),))
    return {"field_draws": field_draws, "chol_vectors": chol_vectors, "rotated_vectors": rotated_vectors, "walkers": walkers}


def block_energy(rotated_block, dual_cols):
    rows = jnp.dot(rotated_block.reshape(-1, ORB).astype(jnp.float32), dual_cols.astype(jnp.float32), preferred_element_type=jnp.float32)
    tiled = rows.reshape(-1, OCC, WALKERS, OCC)
    return jnp.einsum('giwj,gjwi->w', tiled, tiled)

def reference(field_draws, chol_vectors, rotated_vectors, walkers):
    operators = jnp.dot(field_draws.astype(jnp.float32), chol_vectors.reshape(VECS, ORB * ORB).astype(jnp.float32), preferred_element_type=jnp.float32)
    operators = operators.astype(jnp.bfloat16).reshape(WALKERS, ORB, ORB)
    taylor_term = walkers
    propagated = walkers.astype(jnp.float32)
    for degree in range(1, TERMS + 1):
        applied = jnp.einsum('wpq,wqi->wpi', operators.astype(jnp.float32), taylor_term.astype(jnp.float32))
        taylor_term = (applied / degree).astype(jnp.bfloat16)
        propagated = propagated + taylor_term.astype(jnp.float32)
    correlation = jnp.einsum('wpi,wpj->wij', walkers.astype(jnp.float32), propagated, precision=lax.Precision.HIGHEST)
    dual_t = jnp.linalg.solve(jnp.transpose(correlation, (0, 2, 1)), jnp.transpose(propagated, (0, 2, 1)))
    dual_cols = jnp.transpose(dual_t, (2, 0, 1)).reshape(ORB, WALKERS * OCC).astype(jnp.bfloat16)
    dual_cols = lax.optimization_barrier(dual_cols).astype(jnp.float32)
    blocks = rotated_vectors.reshape(VECS // 16, 16, OCC, ORB)
    sums = lax.map(partial(block_energy, dual_cols=dual_cols), blocks)
    exchange_energy = -0.5 * jnp.sum(sums, axis=0)
    return (propagated, exchange_energy)
```

```python
import functools

import jax
import jax.numpy as jnp
from jax import lax
from jax.experimental import pallas as pl
from jax.experimental.pallas import tpu as pltpu
from jax.sharding import PartitionSpec as P

ORB = 512
OCC = 128
TERMS = 4
SLABS = 64
CHOL = 8
MESH = pl.DeviceIdType.MESH
HIGHEST = lax.Precision.HIGHEST
VMEM = pltpu.VMEM
DMA = pltpu.SemaphoreType.DMA


def here():
    chol = lax.axis_index("chol")
    walk = lax.axis_index("walk")
    return chol, walk


def to(chol, walk):
    return {"chol": chol, "walk": walk}


def gather_kernel(
    draws_ref, chol_hbm, rot_hbm, oper_ref, rall_ref,
    chol_buf, gathered, acc, part, recv, red,
    chol_sem, rot_sem, draw_send, draw_recv, part_send, part_recv,
    row_send, row_recv, x_send, x_recv, sib_send, sib_recv,
):
    chol, walk = here()
    z = walk // 4
    core = walk % 2
    x = chol // 2
    y_hi = chol % 2
    sibling = walk + 1 - 2 * core
    barrier = pltpu.get_barrier_semaphore()

    def greet_walk(i, carry):
        pl.semaphore_signal(barrier, inc=1, device_id=to(chol, (walk + i) % 64), device_id_type=MESH)
        return carry

    def greet_chol(i, carry):
        pl.semaphore_signal(barrier, inc=1, device_id=to((chol + i) % 8, walk), device_id_type=MESH)
        return carry

    lax.fori_loop(1, 64, greet_walk, 0)
    lax.fori_loop(1, 8, greet_chol, 0)
    load_chol = pltpu.make_async_copy(chol_hbm, chol_buf, chol_sem)
    load_chol.start()
    load_rot = pltpu.make_async_copy(rot_hbm, rall_ref.at[x, core], rot_sem)
    load_rot.start()
    slot = (z % 8) * 8 + (z // 8) * 4 + walk % 4
    own_draw = pltpu.make_async_copy(draws_ref, gathered.at[slot], draw_recv)
    own_draw.start()
    pl.semaphore_wait(barrier, 70)

    def send_draw(i, carry):
        pltpu.make_async_remote_copy(
            draws_ref, gathered.at[slot], draw_send, draw_recv,
            device_id=to(chol, (walk + i) % 64), device_id_type=MESH,
        ).start()
        return carry

    lax.fori_loop(1, 64, send_draw, 0)

    load_rot.wait()
    mine = rall_ref.at[x, core]

    def x_copy(i):
        peer = ((x + i) % 4) * 2 + y_hi
        return pltpu.make_async_remote_copy(
            mine, mine, x_send.at[i - 1], x_recv.at[i - 1],
            device_id=to(peer, walk), device_id_type=MESH,
        )

    def sib_copy(i):
        block = rall_ref.at[(x + 4 - i) % 4, core]
        return pltpu.make_async_remote_copy(
            block, block, sib_send.at[i], sib_recv.at[i],
            device_id=to(chol, sibling), device_id_type=MESH,
        )

    for i in (1, 2, 3):
        x_copy(i).start()
    sib_copy(0).start()

    load_chol.wait()
    pltpu.make_async_copy(gathered, gathered, draw_recv).wait()

    draws = gathered[...].reshape(SLABS, 256).astype(jnp.bfloat16)
    draws = jnp.broadcast_to(draws.astype(jnp.float32)[:, None, :], (SLABS, 8, 256))
    draws = draws.reshape(SLABS * 8, 256).astype(jnp.bfloat16)
    same_row = (lax.broadcasted_iota(jnp.int32, (512, 256), 0) % 8) == (
        lax.broadcasted_iota(jnp.int32, (512, 256), 1) % 8
    )
    vec_iota = lax.broadcasted_iota(jnp.int32, (256, 256), 0)
    col_iota = lax.broadcasted_iota(jnp.int32, (256, 256), 1) // 8
    acc[...] = jnp.zeros_like(acc)

    def chunk(i, carry):
        pick = jnp.where(vec_iota == col_iota + i * 32, 1.0, 0.0).astype(jnp.bfloat16)
        spread = jnp.dot(draws, pick, preferred_element_type=jnp.float32)
        spread = jnp.where(same_row, spread, 0.0).astype(jnp.bfloat16)
        rows = pl.ds(pl.multiple_of(i * 256, 256), 256)
        acc[...] += jnp.dot(spread, chol_buf[rows, :], preferred_element_type=jnp.float32)
        return carry

    lax.fori_loop(0, 8, chunk, 0)
    for peer in range(CHOL):
        part[peer] = acc[peer * 64 : peer * 64 + 64, :].astype(jnp.bfloat16)

    def part_copy(i):
        peer = (chol + i) % 8
        return pltpu.make_async_remote_copy(
            part.at[peer], recv.at[i - 1], part_send.at[i - 1], part_recv.at[i - 1],
            device_id=to(peer, walk), device_id_type=MESH,
        )

    for i in range(1, 8):
        part_copy(i).start()
    total = part[chol].astype(jnp.float32)
    for i in range(1, 8):
        part_copy(i).wait_recv()
        total = total + recv[i - 1].astype(jnp.float32)
    red[...] = total.astype(jnp.bfloat16).reshape(8, 8, ORB)

    computes = (z % 8) == chol

    def row_target(j):
        return ((j // 4) * 8 + chol) * 4 + j % 4

    def send_rows(j, carry):
        target = row_target(j)

        @pl.when(target != walk)
        def _():
            pltpu.make_async_remote_copy(
                red.at[j], oper_ref.at[walk], row_send.at[j], row_recv,
                device_id=to(chol, target), device_id_type=MESH,
            ).start()

        @pl.when(target == walk)
        def _():
            pltpu.make_async_copy(red.at[j], oper_ref.at[walk], row_recv).start()

        return carry

    lax.fori_loop(0, 8, send_rows, 0)

    for i in (1, 2, 3):
        x_copy(i).wait_recv()
        sib_copy(i).start()

    @pl.when(computes)
    def _():
        pltpu.make_async_copy(oper_ref, oper_ref, row_recv).wait()

    @pl.when(jnp.logical_not(computes))
    def _():
        oper_ref[...] = jnp.zeros_like(oper_ref)

    def drain_rows(j, carry):
        @pl.when(row_target(j) != walk)
        def _():
            pltpu.make_async_remote_copy(
                red.at[j], oper_ref.at[walk], row_send.at[j], row_recv,
                device_id=to(chol, row_target(j)), device_id_type=MESH,
            ).wait_send()

        return carry

    lax.fori_loop(0, 8, drain_rows, 0)
    sent = gathered.at[pl.ds(0, 63)]
    pltpu.make_async_copy(sent, sent, draw_send).wait()
    for i in range(1, 8):
        part_copy(i).wait_send()
    for i in (1, 2, 3):
        x_copy(i).wait_send()
    for i in range(4):
        sib_copy(i).wait()


def gather(draws, chol_vectors, rotated):
    any_ref = pl.BlockSpec(memory_space=pl.ANY)
    vmem = pl.BlockSpec(memory_space=VMEM)
    return pl.pallas_call(
        gather_kernel,
        out_shape=(
            jax.ShapeDtypeStruct((SLABS, 8, ORB), jnp.bfloat16),
            jax.ShapeDtypeStruct((4, 2, 512, ORB), jnp.bfloat16),
        ),
        in_specs=[vmem, any_ref, any_ref],
        out_specs=(vmem, vmem),
        scratch_shapes=[
            VMEM((2048, ORB), jnp.bfloat16),
            VMEM((SLABS, 1, 256), jnp.float32),
            VMEM((512, ORB), jnp.float32),
            VMEM((CHOL, 64, ORB), jnp.bfloat16),
            VMEM((CHOL - 1, 64, ORB), jnp.bfloat16),
            VMEM((8, 8, ORB), jnp.bfloat16),
            DMA, DMA, DMA, DMA, DMA((7,)), DMA((7,)),
            DMA((8,)), DMA, DMA((3,)), DMA((3,)), DMA((4,)), DMA((4,)),
        ],
        compiler_params=pltpu.CompilerParams(collective_id=0, has_side_effects=True),
        name="gather",
    )(draws, chol_vectors, rotated)


def propagate_kernel(oper_ref, walker_ref, prop_ref, dual_ref, corr):
    walker = walker_ref[...]
    term = walker
    total = walker.astype(jnp.float32)
    oper = oper_ref[...]
    for degree in range(1, TERMS + 1):
        applied = jnp.dot(oper, term, preferred_element_type=jnp.float32)
        term = (applied / degree).astype(jnp.bfloat16)
        total = total + term.astype(jnp.float32)
    prop_ref[...] = total
    corr[...] = lax.dot_general(
        walker.astype(jnp.float32), total, (((0,), (0,)), ((), ())), precision=HIGHEST,
        preferred_element_type=jnp.float32,
    )
    lane = lax.broadcasted_iota(jnp.int32, (OCC, OCC), 1)
    sub = lax.broadcasted_iota(jnp.int32, (OCC, OCC), 0)

    def eliminate(k, carry):
        full = corr[...]
        row = corr[pl.ds(k, 1), :]
        here_lane = lane == k
        column = jnp.sum(jnp.where(here_lane, full, 0.0), axis=1, keepdims=True)
        pivot = jnp.sum(jnp.where(here_lane[0:1], row, 0.0), axis=1, keepdims=True)
        inverse = 1.0 / pivot
        scaled = jnp.where(here_lane[0:1], inverse, row * inverse)
        corr[...] = jnp.where(
            sub == k, scaled, jnp.where(here_lane, 0.0, full) - column * scaled
        )
        return carry

    lax.fori_loop(0, OCC, eliminate, 0)
    dual_ref[...] = jnp.dot(
        total, corr[...], precision=HIGHEST, preferred_element_type=jnp.float32
    ).astype(jnp.bfloat16)


def propagate(operator, walker):
    return pl.pallas_call(
        propagate_kernel,
        out_shape=(
            jax.ShapeDtypeStruct((ORB, OCC), jnp.float32),
            jax.ShapeDtypeStruct((ORB, OCC), jnp.bfloat16),
        ),
        scratch_shapes=[VMEM((OCC, OCC), jnp.float32)],
        name="propagate",
    )(operator, walker)


def energy_kernel(
    prop_in, dual_in, rall_hbm, prop_out, energy_out,
    rall, duals, pieces, collected, answer,
    rall_sem, prop_sem, dual_sem, z_send, near_send, z_recv, y_send, y_recv,
    prop_send, prop_recv, piece_send, piece_recv, final_send, final_recv,
):
    chol, walk = here()
    z = walk // 4
    core = walk % 2
    x = chol // 2
    y = (chol % 2) * 2 + (walk // 2) % 2
    computes = (z % 8) == chol
    barrier = pltpu.get_barrier_semaphore()

    def at(zz, yy):
        return to(x * 2 + yy // 2, zz * 4 + (yy % 2) * 2 + core)

    def greet_plane(i, carry):
        spot = (z * 4 + y + i) % 64
        pl.semaphore_signal(barrier, inc=1, device_id=at(spot // 4, spot % 4), device_id_type=MESH)
        return carry

    def greet_chol(i, carry):
        pl.semaphore_signal(barrier, inc=1, device_id=to((chol + i) % 8, walk), device_id_type=MESH)
        return carry

    lax.fori_loop(1, 64, greet_plane, 0)
    lax.fori_loop(1, 8, greet_chol, 0)
    load_rall = pltpu.make_async_copy(rall_hbm, rall, rall_sem)
    load_rall.start()
    half = z // 8
    own = duals.at[y, half]
    hub = (z % 4) == (chol % 4)

    @pl.when(computes)
    def _():
        keep = pltpu.make_async_copy(dual_in, own, dual_sem)
        keep.start()
        keep.wait()

    pl.semaphore_wait(barrier, 70)

    def far_copy(i):
        return pltpu.make_async_remote_copy(
            own, own, z_send.at[i - 1], z_recv.at[half],
            device_id=at((z + 4 * i) % 16, y), device_id_type=MESH,
        )

    def near_copy(which, step):
        block = duals.at[y, which]
        return pltpu.make_async_remote_copy(
            block, block, near_send.at[which, step], z_recv.at[which],
            device_id=at((z + (1, 2, 15)[step]) % 16, y), device_id_type=MESH,
        )

    def y_copy(which, i):
        block = duals.at[y, which]
        return pltpu.make_async_remote_copy(
            block, block, y_send.at[which, i - 1], y_recv.at[which, i - 1],
            device_id=at(z, (y + i) % 4), device_id_type=MESH,
        )

    def prop_copy(i):
        return pltpu.make_async_remote_copy(
            prop_in, prop_out, prop_send.at[i - 1], prop_recv,
            device_id=to((chol + i) % 8, walk), device_id_type=MESH,
        )

    @pl.when(computes)
    def _():
        for i in (2, 1, 3):
            far_copy(i).start()

    def settle(which):
        block = duals.at[y, which]

        @pl.when(jnp.logical_not(jnp.logical_and(computes, half == which)))
        def _():
            pltpu.make_async_copy(block, block, z_recv.at[which]).wait()

        @pl.when(hub)
        def _():
            for step in range(3):
                near_copy(which, step).start()

        for i in (1, 3, 2):
            y_copy(which, i).start()

    settle(half)
    settle(1 - half)

    @pl.when(computes)
    def _():
        pltpu.make_async_copy(prop_in, prop_out, prop_recv).start()
        for i in range(1, 8):
            prop_copy(i).start()

    load_rall.wait()

    def pair_energy(yy):
        block = jnp.concatenate([duals[yy, 0], duals[yy, 1]], axis=1)
        flipped = jnp.transpose(block)

        def vectors(i, carry):
            first, second = carry
            rows = rall[pl.ds(pl.multiple_of(i * 256, 256), 256), :]
            products = jnp.dot(rows, block, preferred_element_type=jnp.float32)
            swapped = lax.dot_general(
                flipped, rows, (((1,), (1,)), ((), ())), preferred_element_type=jnp.float32
            )
            for g in (0, 128):
                one = products[g : g + 128, 0:128] * swapped[0:128, g : g + 128]
                two = products[g : g + 128, 128:256] * swapped[128:256, g : g + 128]
                first = first + jnp.sum(one.reshape(16, 8, 128), axis=0)
                second = second + jnp.sum(two.reshape(16, 8, 128), axis=0)
            return first, second

        zero = jnp.zeros((8, 128), jnp.float32)
        first, second = lax.fori_loop(0, 16, vectors, (zero, zero))
        pieces[yy, 0] = first
        pieces[yy, 1] = second

    def piece_copy(yy, which):
        return pltpu.make_async_remote_copy(
            pieces.at[yy, which], collected.at[z * 4 + y], piece_send.at[yy, which], piece_recv,
            device_id=at(which * 8 + 2 * x + yy // 2, yy), device_id_type=MESH,
        )

    def is_me(yy, which):
        return jnp.logical_and(yy == y, z == which * 8 + 2 * x + yy // 2)

    def send_piece(yy, which):
        @pl.when(jnp.logical_not(is_me(yy, which)))
        def _():
            piece_copy(yy, which).start()

        @pl.when(is_me(yy, which))
        def _():
            pltpu.make_async_copy(
                pieces.at[yy, which], collected.at[z * 4 + y], piece_recv
            ).start()

    def each_pair(i, carry):
        yy = (y + 4 - i) % 4

        @pl.when(i > 0)
        def _():
            for which in (0, 1):
                block = duals.at[yy, which]
                pltpu.make_async_copy(block, block, y_recv.at[which, i - 1]).wait()

        pair_energy(yy)
        for which in (0, 1):
            send_piece(yy, which)
        return carry

    lax.fori_loop(0, 4, each_pair, 0)

    def final_copy(i):
        return pltpu.make_async_remote_copy(
            answer.at[0], answer.at[1], final_send.at[i - 1], final_recv,
            device_id=to((chol + i) % 8, walk), device_id_type=MESH,
        )

    @pl.when(computes)
    def _():
        pltpu.make_async_copy(collected, collected, piece_recv).wait()
        lanes = jnp.sum(jnp.sum(collected[...], axis=0), axis=0, keepdims=True)
        value = -0.5 * jnp.sum(lanes, axis=1, keepdims=True)
        answer[0] = jnp.broadcast_to(value, (8, 128))
        for i in range(1, 8):
            final_copy(i).start()
        pltpu.make_async_copy(answer.at[0], answer.at[1], final_recv).start()

    pltpu.make_async_copy(answer.at[1], answer.at[1], final_recv).wait()
    energy_out[...] = answer[1]
    pltpu.make_async_copy(prop_out, prop_out, prop_recv).wait()

    @pl.when(computes)
    def _():
        for i in (1, 2, 3):
            far_copy(i).wait_send()
        for i in range(1, 8):
            prop_copy(i).wait_send()
            final_copy(i).wait_send()

    @pl.when(hub)
    def _():
        for which in (0, 1):
            for step in range(3):
                near_copy(which, step).wait_send()

    for which in (0, 1):
        for i in (1, 2, 3):
            y_copy(which, i).wait_send()
        for yy in range(4):

            @pl.when(jnp.logical_not(is_me(yy, which)))
            def _():
                piece_copy(yy, which).wait_send()


def energy(propagated, dual, rotated):
    any_ref = pl.BlockSpec(memory_space=pl.ANY)
    vmem = pl.BlockSpec(memory_space=VMEM)
    return pl.pallas_call(
        energy_kernel,
        out_shape=(
            jax.ShapeDtypeStruct((ORB, OCC), jnp.float32),
            jax.ShapeDtypeStruct((8, 128), jnp.float32),
        ),
        in_specs=[vmem, vmem, any_ref],
        out_specs=(vmem, vmem),
        scratch_shapes=[
            VMEM((4096, ORB), jnp.bfloat16),
            VMEM((4, 2, ORB, OCC), jnp.bfloat16),
            VMEM((4, 2, 8, 128), jnp.float32),
            VMEM((64, 8, 128), jnp.float32),
            VMEM((2, 8, 128), jnp.float32),
            DMA, DMA, DMA, DMA((3,)), DMA((2, 3)), DMA((2,)), DMA((2, 3)), DMA((2, 3)),
            DMA((7,)), DMA, DMA((4, 2)), DMA, DMA((7,)), DMA,
        ],
        compiler_params=pltpu.CompilerParams(collective_id=1, has_side_effects=True),
        name="energy",
    )(propagated, dual, rotated)


def per_device(field_draws, chol_vectors, rotated_vectors, walkers):
    operator, rotated = gather(
        field_draws.astype(jnp.float32),
        chol_vectors.reshape(256 * 8, ORB),
        rotated_vectors.reshape(512, ORB),
    )
    propagated, dual = propagate(operator.reshape(ORB, ORB), walkers.reshape(ORB, OCC))
    propagated, exchange = energy(propagated, dual, rotated.reshape(4096, ORB))
    return (propagated.reshape(1, ORB, OCC), exchange[0, 0:1])


def solution(mesh):
    return jax.shard_map(
        per_device,
        mesh=mesh,
        in_specs=(
            P("walk", "chol"),
            P("chol", "walk", None),
            P(("chol", "walk"), None, None),
            P("walk", None, None),
        ),
        out_specs=(P("walk", None, None), P("walk")),
        check_vma=False,
    )
```

```python
import functools

import jax
import jax.numpy as jnp
from jax import lax
from jax.experimental import pallas as pl
from jax.experimental.pallas import tpu as pltpu
from jax.sharding import PartitionSpec as P

ORB = 512
OCC = 128
TERMS = 4
SLABS = 64
CHOL = 8
MESH = pl.DeviceIdType.MESH
HIGHEST = lax.Precision.HIGHEST
VMEM = pltpu.VMEM
DMA = pltpu.SemaphoreType.DMA


def here():
    chol = lax.axis_index("chol")
    walk = lax.axis_index("walk")
    return chol, walk


def to(chol, walk):
    return {"chol": chol, "walk": walk}


def invert(corr):
    lane = lax.broadcasted_iota(jnp.int32, (OCC, OCC), 1)
    sub = lax.broadcasted_iota(jnp.int32, (OCC, OCC), 0)
    column_sub = lax.broadcasted_iota(jnp.int32, (OCC, 1), 0)
    row_lane = lax.broadcasted_iota(jnp.int32, (4, OCC), 1)
    row_sub = lax.broadcasted_iota(jnp.int32, (4, OCC), 0)

    def pair_inverse(m):
        (a, b), (c, d) = m
        scale = 1.0 / (a * d - b * c)
        return ((d * scale, -b * scale), (-c * scale, a * scale))

    def mul(m, n):
        return tuple(
            tuple(m[i][0] * n[0][j] + m[i][1] * n[1][j] for j in (0, 1)) for i in (0, 1)
        )

    def add(m, n, sign):
        return tuple(tuple(m[i][j] + sign * n[i][j] for j in (0, 1)) for i in (0, 1))

    def eliminate(k, carry):
        base = k * 4
        full = corr[...]
        panel = corr[pl.ds(base, 4), :]
        columns = [
            jnp.sum(jnp.where(lane == base + j, full, 0.0), axis=1, keepdims=True) for j in range(4)
        ]
        heads = [
            jnp.sum(jnp.where(row_lane == base + j, panel, 0.0), axis=1, keepdims=True)
            for j in range(4)
        ]

        def block(i, j):
            return tuple(
                tuple(heads[2 * j + b][2 * i + a : 2 * i + a + 1, :] for b in (0, 1)) for a in (0, 1)
            )

        top = pair_inverse(block(0, 0))
        right = mul(top, block(0, 1))
        left = mul(block(1, 0), top)
        low = pair_inverse(add(block(1, 1), mul(block(1, 0), right), -1.0))
        low_left = mul(low, left)
        corner = add(top, mul(right, low_left), 1.0)
        high_right = mul(right, low)
        inverse = (
            corner[0] + tuple(-v for v in high_right[0]),
            corner[1] + tuple(-v for v in high_right[1]),
            tuple(-v for v in low_left[0]) + low[0],
            tuple(-v for v in low_left[1]) + low[1],
        )
        in_pivot = jnp.logical_and(row_lane >= base, row_lane < base + 4)
        panel = jnp.where(in_pivot, jnp.where(row_lane == base + row_sub, 1.0, 0.0), panel)
        result = jnp.where(
            jnp.logical_or(
                jnp.logical_and(lane >= base, lane < base + 4),
                jnp.logical_and(sub >= base, sub < base + 4),
            ),
            0.0,
            full,
        )
        pivot_rows = jnp.logical_and(column_sub >= base, column_sub < base + 4)
        for j in range(4):
            scaled = inverse[j][0] * panel[0:1, :]
            for m in range(1, 4):
                scaled = scaled + inverse[j][m] * panel[m : m + 1, :]
            unit = jnp.where(column_sub == base + j, -1.0, 0.0)
            result = result - jnp.where(pivot_rows, unit, columns[j]) * scaled
        corr[...] = result
        return carry

    lax.fori_loop(0, OCC // 4, eliminate, 0)


def step_kernel(
    draws_ref, chol_hbm, rot_hbm, walker_ref, prop_out, energy_out,
    chol_buf, draw_row, gathered, acc, part, recv, red, oper, rall, prop, corr, duals,
    pieces, collected, answer,
    chol_sem, rot_sem, draw_send, draw_recv, part_send, part_recv,
    row_send, row_recv, x_send, x_recv, sib_send, sib_recv,
    z_send, z_recv, y_send, y_recv, prop_send, prop_recv,
    piece_send, piece_recv, final_send, final_recv,
):
    chol, walk = here()
    z = walk // 4
    core = walk % 2
    x = chol // 2
    y_hi = chol % 2
    y = y_hi * 2 + (walk // 2) % 2
    sibling = walk + 1 - 2 * core
    computes = (z % 8) == chol
    barrier = pltpu.get_barrier_semaphore()

    def remote(src, dst, send, recv_sem, device):
        return pltpu.make_async_remote_copy(
            src, dst, send, recv_sem, device_id=device, device_id_type=MESH
        )

    def at(zz, yy):
        return to(x * 2 + yy // 2, zz * 4 + (yy % 2) * 2 + core)

    def greet(device):
        pl.semaphore_signal(barrier, inc=1, device_id=device, device_id_type=MESH)

    def greet_walk(i, carry):
        greet(to(chol, (walk + i) % 64))
        return carry

    def greet_plane(i, carry):
        greet(to(x * 2 + 1 - y_hi, i * 2 + core))
        return carry

    def greet_chol(i, carry):
        greet(to((chol + i) % 8, walk))
        return carry

    lax.fori_loop(1, 64, greet_walk, 0)
    lax.fori_loop(1, 8, greet_chol, 0)
    lax.fori_loop(0, 32, greet_plane, 0)
    load_chol = pltpu.make_async_copy(chol_hbm, chol_buf, chol_sem)
    load_chol.start()
    load_rot = pltpu.make_async_copy(rot_hbm, rall.at[x, core], rot_sem)
    load_rot.start()
    draw_row[...] = draws_ref[...].astype(jnp.float32)
    slot = (z % 8) * 8 + (z // 8) * 4 + walk % 4
    pl.semaphore_wait(barrier, 63 + 7 + 32)

    own_draw = pltpu.make_async_copy(draw_row, gathered.at[slot], draw_recv)
    own_draw.start()

    def send_draw(i, carry):
        remote(
            draw_row, gathered.at[slot], draw_send, draw_recv, to(chol, (walk + i) % 64)
        ).start()
        return carry

    lax.fori_loop(1, 64, send_draw, 0)

    load_rot.wait()

    def x_copy(i):
        mine = rall.at[x, core]
        return remote(
            mine, mine, x_send.at[i - 1], x_recv.at[i - 1], to(((x + i) % 4) * 2 + y_hi, walk)
        )

    def sib_copy(i):
        block = rall.at[(x + 4 - i) % 4, core]
        return remote(block, block, sib_send.at[i], sib_recv.at[i], to(chol, sibling))

    x_copy(1).start()
    x_copy(3).start()
    sib_copy(0).start()

    load_chol.wait()
    pltpu.make_async_copy(gathered, gathered, draw_recv).wait()

    draws = gathered[...].reshape(SLABS, 256)
    draws = jnp.broadcast_to(draws[:, None, :], (SLABS, 8, 256))
    draws = draws.reshape(SLABS * 8, 256).astype(jnp.bfloat16)
    same_row = (lax.broadcasted_iota(jnp.int32, (512, 256), 0) % 8) == (
        lax.broadcasted_iota(jnp.int32, (512, 256), 1) % 8
    )
    vec_iota = lax.broadcasted_iota(jnp.int32, (256, 256), 0)
    col_iota = lax.broadcasted_iota(jnp.int32, (256, 256), 1) // 8
    acc[...] = jnp.zeros_like(acc)

    def chunk(i, carry):
        pick = jnp.where(vec_iota == col_iota + i * 32, 1.0, 0.0).astype(jnp.bfloat16)
        spread = jnp.dot(draws, pick, preferred_element_type=jnp.float32)
        spread = jnp.where(same_row, spread, 0.0).astype(jnp.bfloat16)
        rows = pl.ds(pl.multiple_of(i * 256, 256), 256)
        acc[...] += jnp.dot(spread, chol_buf[rows, :], preferred_element_type=jnp.float32)
        return carry

    lax.fori_loop(0, 8, chunk, 0)
    for peer in range(CHOL):
        part[peer] = acc[peer * 64 : peer * 64 + 64, :].astype(jnp.bfloat16)

    def part_copy(i):
        peer = (chol + i) % 8
        return remote(
            part.at[peer], recv.at[i - 1], part_send.at[i - 1], part_recv.at[i - 1], to(peer, walk)
        )

    for i in range(1, 8):
        part_copy(i).start()
    total = acc[pl.ds(pl.multiple_of(chol * 64, 64), 64), :]
    for i in range(1, 8):
        part_copy(i).wait_recv()
        total = total + recv[i - 1].astype(jnp.float32)
    red[...] = total.astype(jnp.bfloat16).reshape(8, 8, ORB)

    def row_target(j):
        return ((j // 4) * 8 + chol) * 4 + j % 4

    def row_copy(j):
        return remote(
            red.at[j], oper.at[walk], row_send.at[j], row_recv, to(chol, row_target(j))
        )

    def send_rows(j, carry):
        @pl.when(row_target(j) != walk)
        def _():
            row_copy(j).start()

        @pl.when(row_target(j) == walk)
        def _():
            pltpu.make_async_copy(red.at[j], oper.at[walk], row_recv).start()

        return carry

    lax.fori_loop(0, 8, send_rows, 0)
    x_copy(2).start()
    for i in (1, 3):
        x_copy(i).wait_recv()
        sib_copy(i).start()

    @pl.when(computes)
    def _():
        pltpu.make_async_copy(oper, oper, row_recv).wait()
        walker = walker_ref[...]
        term = walker
        summed = walker.astype(jnp.float32)
        operator = oper[...].reshape(ORB, ORB)
        for degree in range(1, TERMS + 1):
            applied = jnp.dot(operator, term, preferred_element_type=jnp.float32)
            term = (applied / degree).astype(jnp.bfloat16)
            summed = summed + term.astype(jnp.float32)
        prop[...] = summed
        corr[...] = lax.dot_general(
            walker.astype(jnp.float32), summed, (((0,), (0,)), ((), ())), precision=HIGHEST,
            preferred_element_type=jnp.float32,
        )
        invert(corr)
        duals[y, z // 8] = jnp.dot(
            prop[...], corr[...], precision=HIGHEST, preferred_element_type=jnp.float32
        ).astype(jnp.bfloat16)

    def hop(which, kind):
        block = duals.at[y, which]
        return remote(
            block, block, z_send.at[which, kind], z_recv.at[which],
            at((z + (4, 12, 1, 15)[kind]) % 16, y),
        )

    def away(which):
        return (z + 16 - which * 8 - chol) % 16

    def any_of(value, options):
        found = value == options[0]
        for option in options[1:]:
            found = jnp.logical_or(found, value == option)
        return found

    def hops(which):
        d = away(which)
        return (
            jnp.logical_or(d == 0, jnp.logical_and(d == 4, core == 0)),
            jnp.logical_or(d == 0, jnp.logical_and(d == 12, core == 1)),
            any_of(d, (0, 1, 4, 5, 8, 12)),
            any_of(d, (0, 15, 4, 12, 11, 8)),
        )

    def y_copy(which, i):
        block = duals.at[y, which]
        return remote(
            block, block, y_send.at[which, i - 1], y_recv.at[which, i - 1], at(z, (y + i) % 4)
        )

    step = 1 + 2 * core

    def y_relay(which):
        block = duals.at[(y + 4 - step) % 4, which]
        return remote(
            block, block, y_send.at[which, 1], y_recv.at[which, 1], at(z, (y + step) % 4)
        )

    def settle(which):
        block = duals.at[y, which]

        @pl.when(away(which) != 0)
        def _():
            pltpu.make_async_copy(block, block, z_recv.at[which]).wait()

        for kind, condition in enumerate(hops(which)):

            @pl.when(condition)
            def _():
                hop(which, kind).start()

        y_copy(which, 1).start()
        y_copy(which, 3).start()

    def pass_on(which):
        block = duals.at[(y + 4 - step) % 4, which]
        pltpu.make_async_copy(block, block, y_recv.at[which, step - 1]).wait()
        y_relay(which).start()

    d = away(0)
    first = jnp.where(jnp.logical_or(d <= 4, d >= 12), 0, 1)
    settle(first)
    x_copy(2).wait_recv()
    sib_copy(2).start()
    pass_on(first)
    settle(1 - first)
    pass_on(1 - first)

    def prop_copy(i):
        return remote(prop, prop_out, prop_send.at[i - 1], prop_recv, to((chol + i) % 8, walk))

    @pl.when(computes)
    def _():
        for i in range(1, 8):
            prop_copy(i).start()
        pltpu.make_async_copy(prop, prop_out, prop_recv).start()

    for i in range(4):
        sib_copy(i).wait_recv()

    def pair_energy(yy):
        block = jnp.concatenate([duals[yy, 0], duals[yy, 1]], axis=1)
        flipped = jnp.transpose(block)

        def vectors(i, carry):
            one_sum, two_sum = carry
            rows = rall[i // 4, (i // 2) % 2, pl.ds(pl.multiple_of((i % 2) * 256, 256), 256), :]
            products = jnp.dot(rows, block, preferred_element_type=jnp.float32)
            swapped = lax.dot_general(
                flipped, rows, (((1,), (1,)), ((), ())), preferred_element_type=jnp.float32
            )
            for g in (0, 128):
                one = products[g : g + 128, 0:128] * swapped[0:128, g : g + 128]
                two = products[g : g + 128, 128:256] * swapped[128:256, g : g + 128]
                one_sum = one_sum + jnp.sum(one.reshape(16, 8, 128), axis=0)
                two_sum = two_sum + jnp.sum(two.reshape(16, 8, 128), axis=0)
            return one_sum, two_sum

        zero = jnp.zeros((8, 128), jnp.float32)
        one_sum, two_sum = lax.fori_loop(0, 16, vectors, (zero, zero))
        pieces[yy, 0] = one_sum
        pieces[yy, 1] = two_sum

    def piece_copy(yy, which):
        return remote(
            pieces.at[yy, which], collected.at[z * 4 + y], piece_send.at[yy, which], piece_recv,
            at(which * 8 + 2 * x + yy // 2, yy),
        )

    def is_me(yy, which):
        return jnp.logical_and(yy == y, z == which * 8 + 2 * x + yy // 2)

    def send_piece(yy, which):
        @pl.when(jnp.logical_not(is_me(yy, which)))
        def _():
            piece_copy(yy, which).start()

        @pl.when(is_me(yy, which))
        def _():
            pltpu.make_async_copy(
                pieces.at[yy, which], collected.at[z * 4 + y], piece_recv
            ).start()

    def each_pair(n, carry):
        i = jnp.where(n == 2, 3, jnp.where(n == 3, 2, n))
        yy = (y + 4 - i) % 4

        @pl.when(jnp.logical_and(n > 0, i != step))
        def _():
            for which in (0, 1):
                block = duals.at[yy, which]
                pltpu.make_async_copy(block, block, y_recv.at[which, i - 1]).wait()

        pair_energy(yy)
        for which in (0, 1):
            send_piece(yy, which)
        return carry

    lax.fori_loop(0, 4, each_pair, 0)

    def final_copy(i):
        return remote(
            answer.at[0], answer.at[1], final_send.at[i - 1], final_recv, to((chol + i) % 8, walk)
        )

    @pl.when(computes)
    def _():
        pltpu.make_async_copy(collected, collected, piece_recv).wait()
        lanes = jnp.sum(jnp.sum(collected[...], axis=0), axis=0, keepdims=True)
        value = -0.5 * jnp.sum(lanes, axis=1, keepdims=True)
        answer[0] = jnp.broadcast_to(value, (8, 128))
        for i in range(1, 8):
            final_copy(i).start()
        pltpu.make_async_copy(answer.at[0], answer.at[1], final_recv).start()

    def drain_rows(j, carry):
        @pl.when(row_target(j) != walk)
        def _():
            row_copy(j).wait_send()

        return carry

    lax.fori_loop(0, 8, drain_rows, 0)
    sent = gathered.at[pl.ds(0, 63)]
    pltpu.make_async_copy(sent, sent, draw_send).wait()
    for i in range(1, 8):
        part_copy(i).wait_send()
    for i in (1, 2, 3):
        x_copy(i).wait_send()
    for i in range(4):
        sib_copy(i).wait_send()
    for which in (0, 1):
        for kind, condition in enumerate(hops(which)):

            @pl.when(condition)
            def _():
                hop(which, kind).wait_send()

        y_copy(which, 1).wait_send()
        y_copy(which, 3).wait_send()
        y_relay(which).wait_send()
        for yy in range(4):

            @pl.when(jnp.logical_not(is_me(yy, which)))
            def _():
                piece_copy(yy, which).wait_send()

    pltpu.make_async_copy(prop_out, prop_out, prop_recv).wait()

    @pl.when(computes)
    def _():
        for i in range(1, 8):
            prop_copy(i).wait_send()
            final_copy(i).wait_send()

    pltpu.make_async_copy(answer.at[1], answer.at[1], final_recv).wait()
    energy_out[...] = answer[1]


def per_device(field_draws, chol_vectors, rotated_vectors, walkers):
    any_ref = pl.BlockSpec(memory_space=pl.ANY)
    vmem = pl.BlockSpec(memory_space=VMEM)
    propagated, exchange = pl.pallas_call(
        step_kernel,
        out_shape=(
            jax.ShapeDtypeStruct((ORB, OCC), jnp.float32),
            jax.ShapeDtypeStruct((8, 128), jnp.float32),
        ),
        in_specs=[vmem, any_ref, any_ref, vmem],
        out_specs=(vmem, vmem),
        scratch_shapes=[
            VMEM((2048, ORB), jnp.bfloat16),
            VMEM((1, 256), jnp.float32),
            VMEM((SLABS, 1, 256), jnp.float32),
            VMEM((512, ORB), jnp.float32),
            VMEM((CHOL, 64, ORB), jnp.bfloat16),
            VMEM((CHOL - 1, 64, ORB), jnp.bfloat16),
            VMEM((8, 8, ORB), jnp.bfloat16),
            VMEM((SLABS, 8, ORB), jnp.bfloat16),
            VMEM((4, 2, 512, ORB), jnp.bfloat16),
            VMEM((ORB, OCC), jnp.float32),
            VMEM((OCC, OCC), jnp.float32),
            VMEM((4, 2, ORB, OCC), jnp.bfloat16),
            VMEM((4, 2, 8, 128), jnp.float32),
            VMEM((64, 8, 128), jnp.float32),
            VMEM((2, 8, 128), jnp.float32),
            DMA, DMA, DMA, DMA, DMA((7,)), DMA((7,)),
            DMA((8,)), DMA, DMA((3,)), DMA((3,)), DMA((4,)), DMA((4,)),
            DMA((2, 4)), DMA((2,)), DMA((2, 3)), DMA((2, 3)), DMA((7,)), DMA,
            DMA((4, 2)), DMA, DMA((7,)), DMA,
        ],
        compiler_params=pltpu.CompilerParams(collective_id=0, has_side_effects=True),
        name="step",
    )(
        field_draws,
        chol_vectors.reshape(256 * 8, ORB),
        rotated_vectors.reshape(512, ORB),
        walkers.reshape(ORB, OCC),
    )
    return (propagated.reshape(1, ORB, OCC), exchange[0, 0:1])


def solution(mesh):
    return jax.shard_map(
        per_device,
        mesh=mesh,
        in_specs=(
            P("walk", "chol"),
            P("chol", "walk", None),
            P(("chol", "walk"), None, None),
            P("walk", None, None),
        ),
        out_specs=(P("walk", None, None), P("walk")),
        check_vma=False,
    )
```

```python
import functools

import jax
import jax.numpy as jnp
from jax import lax
from jax.experimental import pallas as pl
from jax.experimental.pallas import tpu as pltpu
from jax.sharding import PartitionSpec as P

ORB = 512
OCC = 128
TERMS = 4
SLABS = 64
CHOL = 8
MESH = pl.DeviceIdType.MESH
HIGHEST = lax.Precision.HIGHEST
VMEM = pltpu.VMEM
DMA = pltpu.SemaphoreType.DMA


def here():
    chol = lax.axis_index("chol")
    walk = lax.axis_index("walk")
    return chol, walk


def to(chol, walk):
    return {"chol": chol, "walk": walk}


def invert(corr):
    lane = lax.broadcasted_iota(jnp.int32, (8, OCC), 1)
    sub = lax.broadcasted_iota(jnp.int32, (8, OCC), 0)

    def pair_inverse(m):
        (a, b), (c, d) = m
        scale = 1.0 / (a * d - b * c)
        return ((d * scale, -b * scale), (-c * scale, a * scale))

    def mul(m, n):
        return tuple(
            tuple(m[i][0] * n[0][j] + m[i][1] * n[1][j] for j in (0, 1)) for i in (0, 1)
        )

    def add(m, n, sign):
        return tuple(tuple(m[i][j] + sign * n[i][j] for j in (0, 1)) for i in (0, 1))

    def pivots(full, p):
        columns = [
            jnp.broadcast_to(full[:, p + j : p + j + 1], (OCC, OCC)).reshape(16, 8, OCC)
            for j in range(4)
        ]

        def block(i, j):
            return tuple(
                tuple(
                    jnp.broadcast_to(
                        columns[2 * j + b][0, p + 2 * i + a : p + 2 * i + a + 1, :], (8, OCC)
                    )
                    for b in (0, 1)
                )
                for a in (0, 1)
            )

        top = pair_inverse(block(0, 0))
        right = mul(top, block(0, 1))
        left = mul(block(1, 0), top)
        low = pair_inverse(add(block(1, 1), mul(block(1, 0), right), -1.0))
        low_left = mul(low, left)
        corner = add(top, mul(right, low_left), 1.0)
        high_right = mul(right, low)
        inverse = (
            corner[0] + tuple(-v for v in high_right[0]),
            corner[1] + tuple(-v for v in high_right[1]),
            tuple(-v for v in low_left[0]) + low[0],
            tuple(-v for v in low_left[1]) + low[1],
        )
        in_pivot = jnp.logical_and(lane >= p, lane < p + 4)
        rows = []
        for m in range(4):
            row = jnp.broadcast_to(full[p + m : p + m + 1, :], (8, OCC))
            rows.append(jnp.where(in_pivot, jnp.where(lane == p + m, 1.0, 0.0), row))
        result = jnp.where(in_pivot[None], 0.0, full.reshape(16, 8, OCC))
        scaled = []
        for j in range(4):
            line = inverse[j][0] * rows[0]
            for m in range(1, 4):
                line = line + inverse[j][m] * rows[m]
            scaled.append(line)
            result = result - columns[j] * line[None]
        head = result[0]
        for j in range(4):
            head = jnp.where(sub == p + j, scaled[j], head)
        return jnp.concatenate([head, result[1:].reshape(OCC - 8, OCC)], axis=0)

    def eliminate(k, carry):
        full = pivots(pivots(corr[...], 0), 4)
        full = pltpu.roll(full, OCC - 8, 1)
        corr[0 : OCC - 8, :] = full[8:, :]
        corr[OCC - 8 :, :] = full[0:8, :]
        return carry

    lax.fori_loop(0, OCC // 8, eliminate, 0)


def step_kernel(
    draws_ref, chol_hbm, rot_hbm, walker_ref, prop_out, energy_out,
    chol_buf, draw_row, gathered, spreads, acc, part, recv, red, oper, rall, prop, corr, duals,
    pieces, collected, answer,
    chol_sem, rot_sem, draw_send, draw_recv, part_send, part_recv,
    row_send, row_recv, x_send, x_recv, sib_send, sib_recv,
    z_send, z_recv, y_send, y_recv, prop_send, prop_recv,
    piece_send, piece_recv, final_send, final_recv,
):
    chol, walk = here()
    z = walk // 4
    core = walk % 2
    x = chol // 2
    y_hi = chol % 2
    y = y_hi * 2 + (walk // 2) % 2
    sibling = walk + 1 - 2 * core
    computes = (z % 8) == chol
    barrier = pltpu.get_barrier_semaphore()

    def remote(src, dst, send, recv_sem, device):
        return pltpu.make_async_remote_copy(
            src, dst, send, recv_sem, device_id=device, device_id_type=MESH
        )

    def at(zz, yy):
        return to(x * 2 + yy // 2, zz * 4 + (yy % 2) * 2 + core)

    def greet(device):
        pl.semaphore_signal(barrier, inc=1, device_id=device, device_id_type=MESH)

    def greet_walk(i, carry):
        greet(to(chol, (walk + i) % 64))
        return carry

    def greet_plane(i, carry):
        greet(to(x * 2 + 1 - y_hi, i * 2 + core))
        return carry

    def greet_chol(i, carry):
        greet(to((chol + i) % 8, walk))
        return carry

    lax.fori_loop(1, 64, greet_walk, 0)
    lax.fori_loop(1, 8, greet_chol, 0)
    lax.fori_loop(0, 32, greet_plane, 0)
    load_chol = pltpu.make_async_copy(chol_hbm, chol_buf, chol_sem)
    load_chol.start()
    load_rot = pltpu.make_async_copy(rot_hbm, rall.at[x, core], rot_sem)
    load_rot.start()
    draw_row[...] = draws_ref[...].astype(jnp.float32)
    slot = (z % 8) * 8 + (z // 8) * 4 + walk % 4
    pl.semaphore_wait(barrier, 63 + 7 + 32)

    own_draw = pltpu.make_async_copy(draw_row, gathered.at[slot], draw_recv)
    own_draw.start()

    def send_draw(i, carry):
        remote(
            draw_row, gathered.at[slot], draw_send, draw_recv, to(chol, (walk + i) % 64)
        ).start()
        return carry

    lax.fori_loop(1, 64, send_draw, 0)

    load_rot.wait()

    def x_copy(i):
        mine = rall.at[x, core]
        return remote(
            mine, mine, x_send.at[i - 1], x_recv.at[i - 1], to(((x + i) % 4) * 2 + y_hi, walk)
        )

    def sib_copy(i):
        block = rall.at[(x + 4 - i) % 4, core]
        return remote(block, block, sib_send.at[i], sib_recv.at[i], to(chol, sibling))

    x_copy(1).start()
    x_copy(3).start()
    sib_copy(0).start()

    load_chol.wait()
    pltpu.make_async_copy(gathered, gathered, draw_recv).wait()

    draws = gathered[...].reshape(SLABS, 256)
    draws = jnp.broadcast_to(draws[:, None, :], (SLABS, 8, 256))
    draws = draws.reshape(SLABS * 8, 256).astype(jnp.bfloat16)
    same_row = (lax.broadcasted_iota(jnp.int32, (512, 256), 0) % 8) == (
        lax.broadcasted_iota(jnp.int32, (512, 256), 1) % 8
    )
    vec_iota = lax.broadcasted_iota(jnp.int32, (256, 256), 0)
    col_iota = lax.broadcasted_iota(jnp.int32, (256, 256), 1) // 8

    def chunk(i, carry):
        pick = jnp.where(vec_iota == col_iota + i * 32, 1.0, 0.0).astype(jnp.bfloat16)
        spread = jnp.dot(draws, pick, preferred_element_type=jnp.float32)
        columns = pl.ds(pl.multiple_of(i * 256, 256), 256)
        spreads[:, columns] = jnp.where(same_row, spread, 0.0).astype(jnp.bfloat16)
        return carry

    lax.fori_loop(0, 8, chunk, 0)

    def part_copy(n, i):
        peer = (chol + i) % 8
        return remote(
            part.at[n, peer], recv.at[n, i - 1], part_send.at[n, i - 1], part_recv.at[n, i - 1],
            to(peer, walk),
        )

    for n in range(2):
        terms = jnp.dot(
            spreads[...], chol_buf[:, n * 256 : n * 256 + 256], preferred_element_type=jnp.float32
        )
        acc[n] = terms
        part[n] = terms.astype(jnp.bfloat16).reshape(CHOL, 64, 256)
        for i in range(1, 8):
            part_copy(n, i).start()
    for n in range(2):
        total = acc[n, pl.ds(pl.multiple_of(chol * 64, 64), 64), :]
        for i in range(1, 8):
            part_copy(n, i).wait_recv()
            total = total + recv[n, i - 1].astype(jnp.float32)
        red[:, :, n * 256 : n * 256 + 256] = total.astype(jnp.bfloat16).reshape(8, 8, 256)

    def row_target(j):
        return ((j // 4) * 8 + chol) * 4 + j % 4

    def row_copy(j):
        return remote(
            red.at[j], oper.at[walk], row_send.at[j], row_recv, to(chol, row_target(j))
        )

    def send_rows(j, carry):
        @pl.when(row_target(j) != walk)
        def _():
            row_copy(j).start()

        @pl.when(row_target(j) == walk)
        def _():
            pltpu.make_async_copy(red.at[j], oper.at[walk], row_recv).start()

        return carry

    lax.fori_loop(0, 8, send_rows, 0)
    x_copy(2).start()
    for i in (1, 3):
        x_copy(i).wait_recv()
        sib_copy(i).start()

    @pl.when(computes)
    def _():
        pltpu.make_async_copy(oper, oper, row_recv).wait()
        walker = walker_ref[...]
        term = walker
        summed = walker.astype(jnp.float32)
        operator = oper[...].reshape(ORB, ORB)
        for degree in range(1, TERMS + 1):
            applied = jnp.dot(operator, term, preferred_element_type=jnp.float32)
            term = (applied / degree).astype(jnp.bfloat16)
            summed = summed + term.astype(jnp.float32)
        prop[...] = summed
        corr[...] = lax.dot_general(
            walker.astype(jnp.float32), summed, (((0,), (0,)), ((), ())), precision=HIGHEST,
            preferred_element_type=jnp.float32,
        )
        invert(corr)
        duals[y, z // 8] = jnp.dot(
            prop[...], corr[...], precision=HIGHEST, preferred_element_type=jnp.float32
        ).astype(jnp.bfloat16)

    def hop(which, kind):
        block = duals.at[y, which]
        return remote(
            block, block, z_send.at[which, kind], z_recv.at[which],
            at((z + (4, 12, 1, 15)[kind]) % 16, y),
        )

    def away(which):
        return (z + 16 - which * 8 - chol) % 16

    def any_of(value, options):
        found = value == options[0]
        for option in options[1:]:
            found = jnp.logical_or(found, value == option)
        return found

    def hops(which):
        d = away(which)
        return (
            jnp.logical_or(d == 0, jnp.logical_and(d == 4, core == 0)),
            jnp.logical_or(d == 0, jnp.logical_and(d == 12, core == 1)),
            any_of(d, (0, 1, 4, 5, 8, 12)),
            any_of(d, (0, 15, 4, 12, 11, 8)),
        )

    def y_copy(which, i):
        block = duals.at[y, which]
        return remote(
            block, block, y_send.at[which, i - 1], y_recv.at[which, i - 1], at(z, (y + i) % 4)
        )

    step = 1 + 2 * core

    def y_relay(which):
        block = duals.at[(y + 4 - step) % 4, which]
        return remote(
            block, block, y_send.at[which, 1], y_recv.at[which, 1], at(z, (y + step) % 4)
        )

    def settle(which):
        block = duals.at[y, which]

        @pl.when(away(which) != 0)
        def _():
            pltpu.make_async_copy(block, block, z_recv.at[which]).wait()

        for kind, condition in enumerate(hops(which)):

            @pl.when(condition)
            def _():
                hop(which, kind).start()

        y_copy(which, 1).start()
        y_copy(which, 3).start()

    def pass_on(which):
        block = duals.at[(y + 4 - step) % 4, which]
        pltpu.make_async_copy(block, block, y_recv.at[which, step - 1]).wait()
        y_relay(which).start()

    d = away(0)
    first = jnp.where(jnp.logical_or(d <= 4, d >= 12), 0, 1)
    settle(first)
    settle(1 - first)
    pass_on(first)
    x_copy(2).wait_recv()
    sib_copy(2).start()
    pass_on(1 - first)

    def prop_copy(i):
        return remote(prop, prop_out, prop_send.at[i - 1], prop_recv, to((chol + i) % 8, walk))

    @pl.when(computes)
    def _():
        for i in range(1, 8):
            prop_copy(i).start()
        pltpu.make_async_copy(prop, prop_out, prop_recv).start()

    for i in range(4):
        sib_copy(i).wait_recv()

    def pair_energy(yy):
        block = jnp.concatenate([duals[yy, 0], duals[yy, 1]], axis=1)

        def vectors(i, sums):
            rows = rall[i].reshape(1024, ORB)
            products = jnp.dot(rows, block, preferred_element_type=jnp.float32)
            sums = list(sums)
            for g in range(8):
                for w in range(2):
                    one = products[g * 128 : g * 128 + 128, w * 128 : w * 128 + 128]
                    swapped = jnp.transpose(one.astype(jnp.bfloat16)).astype(jnp.float32)
                    terms = (one * swapped).reshape(16, 8, 128)
                    sums[w] = sums[w] + jnp.sum(terms, axis=0)
            return tuple(sums)

        zero = jnp.zeros((8, 128), jnp.float32)
        sums = lax.fori_loop(0, 4, vectors, (zero, zero))
        pieces[yy, 0] = sums[0]
        pieces[yy, 1] = sums[1]

    def piece_copy(yy, which):
        return remote(
            pieces.at[yy, which], collected.at[z * 4 + y], piece_send.at[yy, which], piece_recv,
            at(which * 8 + 2 * x + yy // 2, yy),
        )

    def is_me(yy, which):
        return jnp.logical_and(yy == y, z == which * 8 + 2 * x + yy // 2)

    def send_piece(yy, which):
        @pl.when(jnp.logical_not(is_me(yy, which)))
        def _():
            piece_copy(yy, which).start()

        @pl.when(is_me(yy, which))
        def _():
            pltpu.make_async_copy(
                pieces.at[yy, which], collected.at[z * 4 + y], piece_recv
            ).start()

    def each_pair(n, carry):
        i = jnp.where(n == 2, 3, jnp.where(n == 3, 2, n))
        yy = (y + 4 - i) % 4

        @pl.when(jnp.logical_and(n > 0, i != step))
        def _():
            for which in (0, 1):
                block = duals.at[yy, which]
                pltpu.make_async_copy(block, block, y_recv.at[which, i - 1]).wait()

        pair_energy(yy)
        for which in (0, 1):
            send_piece(yy, which)
        return carry

    lax.fori_loop(0, 4, each_pair, 0)

    def final_copy(i):
        return remote(
            answer.at[0], answer.at[1], final_send.at[i - 1], final_recv, to((chol + i) % 8, walk)
        )

    @pl.when(computes)
    def _():
        pltpu.make_async_copy(collected, collected, piece_recv).wait()
        lanes = jnp.sum(jnp.sum(collected[...], axis=0), axis=0, keepdims=True)
        value = -0.5 * jnp.sum(lanes, axis=1, keepdims=True)
        answer[0] = jnp.broadcast_to(value, (8, 128))
        for i in range(1, 8):
            final_copy(i).start()
        pltpu.make_async_copy(answer.at[0], answer.at[1], final_recv).start()

    def drain_rows(j, carry):
        @pl.when(row_target(j) != walk)
        def _():
            row_copy(j).wait_send()

        return carry

    lax.fori_loop(0, 8, drain_rows, 0)
    sent = gathered.at[pl.ds(0, 63)]
    pltpu.make_async_copy(sent, sent, draw_send).wait()
    for n in range(2):
        for i in range(1, 8):
            part_copy(n, i).wait_send()
    for i in (1, 2, 3):
        x_copy(i).wait_send()
    for i in range(4):
        sib_copy(i).wait_send()
    for which in (0, 1):
        for kind, condition in enumerate(hops(which)):

            @pl.when(condition)
            def _():
                hop(which, kind).wait_send()

        y_copy(which, 1).wait_send()
        y_copy(which, 3).wait_send()
        y_relay(which).wait_send()
        for yy in range(4):

            @pl.when(jnp.logical_not(is_me(yy, which)))
            def _():
                piece_copy(yy, which).wait_send()

    pltpu.make_async_copy(prop_out, prop_out, prop_recv).wait()

    @pl.when(computes)
    def _():
        for i in range(1, 8):
            prop_copy(i).wait_send()
            final_copy(i).wait_send()

    pltpu.make_async_copy(answer.at[1], answer.at[1], final_recv).wait()
    energy_out[...] = answer[1]


def per_device(field_draws, chol_vectors, rotated_vectors, walkers):
    any_ref = pl.BlockSpec(memory_space=pl.ANY)
    vmem = pl.BlockSpec(memory_space=VMEM)
    propagated, exchange = pl.pallas_call(
        step_kernel,
        out_shape=(
            jax.ShapeDtypeStruct((ORB, OCC), jnp.float32),
            jax.ShapeDtypeStruct((8, 128), jnp.float32),
        ),
        in_specs=[vmem, any_ref, any_ref, vmem],
        out_specs=(vmem, vmem),
        scratch_shapes=[
            VMEM((2048, ORB), jnp.bfloat16),
            VMEM((1, 256), jnp.float32),
            VMEM((SLABS, 1, 256), jnp.float32),
            VMEM((512, 2048), jnp.bfloat16),
            VMEM((2, 512, 256), jnp.float32),
            VMEM((2, CHOL, 64, 256), jnp.bfloat16),
            VMEM((2, CHOL - 1, 64, 256), jnp.bfloat16),
            VMEM((8, 8, ORB), jnp.bfloat16),
            VMEM((SLABS, 8, ORB), jnp.bfloat16),
            VMEM((4, 2, 512, ORB), jnp.bfloat16),
            VMEM((ORB, OCC), jnp.float32),
            VMEM((OCC, OCC), jnp.float32),
            VMEM((4, 2, ORB, OCC), jnp.bfloat16),
            VMEM((4, 2, 8, 128), jnp.float32),
            VMEM((64, 8, 128), jnp.float32),
            VMEM((2, 8, 128), jnp.float32),
            DMA, DMA, DMA, DMA, DMA((2, 7)), DMA((2, 7)),
            DMA((8,)), DMA, DMA((3,)), DMA((3,)), DMA((4,)), DMA((4,)),
            DMA((2, 4)), DMA((2,)), DMA((2, 3)), DMA((2, 3)), DMA((7,)), DMA,
            DMA((4, 2)), DMA, DMA((7,)), DMA,
        ],
        compiler_params=pltpu.CompilerParams(collective_id=0, has_side_effects=True),
        name="step",
    )(
        field_draws,
        chol_vectors.reshape(256 * 8, ORB),
        rotated_vectors.reshape(512, ORB),
        walkers.reshape(ORB, OCC),
    )
    return (propagated.reshape(1, ORB, OCC), exchange[0, 0:1])


def solution(mesh):
    return jax.shard_map(
        per_device,
        mesh=mesh,
        in_specs=(
            P("walk", "chol"),
            P("chol", "walk", None),
            P(("chol", "walk"), None, None),
            P("walk", None, None),
        ),
        out_specs=(P("walk", None, None), P("walk")),
        check_vma=False,
    )
```

```python
import functools

import jax
import jax.numpy as jnp
from jax import lax
from jax.experimental import pallas as pl
from jax.experimental.pallas import tpu as pltpu
from jax.sharding import PartitionSpec as P

ORB = 512
OCC = 128
TERMS = 4
SLABS = 64
CHOL = 8
MESH = pl.DeviceIdType.MESH
HIGHEST = lax.Precision.HIGHEST
VMEM = pltpu.VMEM
DMA = pltpu.SemaphoreType.DMA


def here():
    chol = lax.axis_index("chol")
    walk = lax.axis_index("walk")
    return chol, walk


def to(chol, walk):
    return {"chol": chol, "walk": walk}


def invert(corr):
    lane = lax.broadcasted_iota(jnp.int32, (8, OCC), 1)
    sub = lax.broadcasted_iota(jnp.int32, (8, OCC), 0)

    def pair_inverse(m):
        (a, b), (c, d) = m
        scale = 1.0 / (a * d - b * c)
        return ((d * scale, -b * scale), (-c * scale, a * scale))

    def mul(m, n):
        return tuple(
            tuple(m[i][0] * n[0][j] + m[i][1] * n[1][j] for j in (0, 1)) for i in (0, 1)
        )

    def add(m, n, sign):
        return tuple(tuple(m[i][j] + sign * n[i][j] for j in (0, 1)) for i in (0, 1))

    def pivots(full, p):
        columns = [
            jnp.broadcast_to(full[:, p + j : p + j + 1], (OCC, OCC)).reshape(16, 8, OCC)
            for j in range(4)
        ]

        def block(i, j):
            return tuple(
                tuple(
                    jnp.broadcast_to(
                        columns[2 * j + b][0, p + 2 * i + a : p + 2 * i + a + 1, :], (8, OCC)
                    )
                    for b in (0, 1)
                )
                for a in (0, 1)
            )

        top = pair_inverse(block(0, 0))
        right = mul(top, block(0, 1))
        left = mul(block(1, 0), top)
        low = pair_inverse(add(block(1, 1), mul(block(1, 0), right), -1.0))
        low_left = mul(low, left)
        corner = add(top, mul(right, low_left), 1.0)
        high_right = mul(right, low)
        inverse = (
            corner[0] + tuple(-v for v in high_right[0]),
            corner[1] + tuple(-v for v in high_right[1]),
            tuple(-v for v in low_left[0]) + low[0],
            tuple(-v for v in low_left[1]) + low[1],
        )
        in_pivot = jnp.logical_and(lane >= p, lane < p + 4)
        rows = []
        for m in range(4):
            row = jnp.broadcast_to(full[p + m : p + m + 1, :], (8, OCC))
            rows.append(jnp.where(in_pivot, jnp.where(lane == p + m, 1.0, 0.0), row))
        result = jnp.where(in_pivot[None], 0.0, full.reshape(16, 8, OCC))
        scaled = []
        for j in range(4):
            line = inverse[j][0] * rows[0]
            for m in range(1, 4):
                line = line + inverse[j][m] * rows[m]
            scaled.append(line)
            result = result - columns[j] * line[None]
        head = result[0]
        for j in range(4):
            head = jnp.where(sub == p + j, scaled[j], head)
        return jnp.concatenate([head, result[1:].reshape(OCC - 8, OCC)], axis=0)

    def eliminate(k, carry):
        full = pivots(pivots(corr[...], 0), 4)
        full = pltpu.roll(full, OCC - 8, 1)
        corr[0 : OCC - 8, :] = full[8:, :]
        corr[OCC - 8 :, :] = full[0:8, :]
        return carry

    lax.fori_loop(0, OCC // 8, eliminate, 0)


def step_kernel(
    draws_ref, chol_hbm, rot_hbm, walker_ref, prop_out, energy_out,
    chol_buf, draw_row, gathered, spreads, acc, part, recv, red, oper, rall, prop, corr, duals,
    pieces, collected,
    chol_sem, rot_sem, draw_send, draw_recv, part_send, part_recv,
    row_send, row_recv, x_send, x_recv, sib_send, sib_recv,
    z_send, z_recv, y_send, y_recv, prop_send, prop_recv,
    piece_send, piece_recv,
):
    chol, walk = here()
    z = walk // 4
    core = walk % 2
    x = chol // 2
    y_hi = chol % 2
    y = y_hi * 2 + (walk // 2) % 2
    sibling = walk + 1 - 2 * core
    computes = (z % 8) == chol
    barrier = pltpu.get_barrier_semaphore()

    def remote(src, dst, send, recv_sem, device):
        return pltpu.make_async_remote_copy(
            src, dst, send, recv_sem, device_id=device, device_id_type=MESH
        )

    def at(zz, yy):
        return to(x * 2 + yy // 2, zz * 4 + (yy % 2) * 2 + core)

    def greet(device):
        pl.semaphore_signal(barrier, inc=1, device_id=device, device_id_type=MESH)

    def greet_walk(i, carry):
        greet(to(chol, (walk + i) % 64))
        return carry

    def greet_plane(i, carry):
        greet(to(x * 2 + 1 - y_hi, i * 2 + core))
        return carry

    def greet_chol(i, carry):
        greet(to((chol + i) % 8, walk))
        return carry

    x_from = (z % 8) // 2

    def greet_pieces(i, carry):
        other_chol = x_from * 2 + i // 32
        other_walk = (i % 32) * 2 + core
        same = jnp.logical_and(other_chol == chol, other_walk == walk)

        @pl.when(jnp.logical_not(same))
        def _():
            greet(to(other_chol, other_walk))

        return carry

    lax.fori_loop(1, 64, greet_walk, 0)
    lax.fori_loop(1, 8, greet_chol, 0)
    lax.fori_loop(0, 32, greet_plane, 0)
    lax.fori_loop(0, 64, greet_pieces, 0)
    load_chol = pltpu.make_async_copy(chol_hbm, chol_buf, chol_sem)
    load_chol.start()
    load_rot = pltpu.make_async_copy(rot_hbm, rall.at[x, core], rot_sem)
    load_rot.start()
    draw_row[...] = draws_ref[...].astype(jnp.float32)
    slot = (z % 8) * 8 + (z // 8) * 4 + walk % 4
    pl.semaphore_wait(barrier, 63 + 7 + 32 + jnp.where(x_from == x, 63, 64))

    own_draw = pltpu.make_async_copy(draw_row, gathered.at[slot], draw_recv)
    own_draw.start()

    def send_draw(i, carry):
        remote(
            draw_row, gathered.at[slot], draw_send, draw_recv, to(chol, (walk + i) % 64)
        ).start()
        return carry

    lax.fori_loop(1, 64, send_draw, 0)

    load_rot.wait()

    def x_copy(i):
        mine = rall.at[x, core]
        return remote(
            mine, mine, x_send.at[i - 1], x_recv.at[i - 1], to(((x + i) % 4) * 2 + y_hi, walk)
        )

    def sib_copy(i):
        block = rall.at[(x + 4 - i) % 4, core]
        return remote(block, block, sib_send.at[i], sib_recv.at[i], to(chol, sibling))

    x_copy(1).start()
    x_copy(3).start()
    sib_copy(0).start()

    load_chol.wait()
    pltpu.make_async_copy(gathered, gathered, draw_recv).wait()

    draws = gathered[...].reshape(SLABS, 256)
    draws = jnp.broadcast_to(draws[:, None, :], (SLABS, 8, 256))
    draws = draws.reshape(SLABS * 8, 256).astype(jnp.bfloat16)
    same_row = (lax.broadcasted_iota(jnp.int32, (512, 256), 0) % 8) == (
        lax.broadcasted_iota(jnp.int32, (512, 256), 1) % 8
    )
    vec_iota = lax.broadcasted_iota(jnp.int32, (256, 256), 0)
    col_iota = lax.broadcasted_iota(jnp.int32, (256, 256), 1) // 8

    def chunk(i, carry):
        pick = jnp.where(vec_iota == col_iota + i * 32, 1.0, 0.0).astype(jnp.bfloat16)
        spread = jnp.dot(draws, pick, preferred_element_type=jnp.float32)
        columns = pl.ds(pl.multiple_of(i * 256, 256), 256)
        spreads[:, columns] = jnp.where(same_row, spread, 0.0).astype(jnp.bfloat16)
        return carry

    lax.fori_loop(0, 8, chunk, 0)

    def part_copy(n, i):
        peer = (chol + i) % 8
        return remote(
            part.at[n, peer], recv.at[n, i - 1], part_send.at[n, i - 1], part_recv.at[n, i - 1],
            to(peer, walk),
        )

    for n in range(2):
        terms = jnp.dot(
            spreads[...], chol_buf[:, n * 256 : n * 256 + 256], preferred_element_type=jnp.float32
        )
        acc[n] = terms
        part[n] = terms.astype(jnp.bfloat16).reshape(CHOL, 64, 256)
        for i in range(1, 8):
            part_copy(n, i).start()
    for n in range(2):
        total = acc[n, pl.ds(pl.multiple_of(chol * 64, 64), 64), :]
        for i in range(1, 8):
            part_copy(n, i).wait_recv()
            total = total + recv[n, i - 1].astype(jnp.float32)
        red[:, :, n * 256 : n * 256 + 256] = total.astype(jnp.bfloat16).reshape(8, 8, 256)

    def row_target(j):
        return ((j // 4) * 8 + chol) * 4 + j % 4

    def row_copy(j):
        return remote(
            red.at[j], oper.at[walk], row_send.at[j], row_recv, to(chol, row_target(j))
        )

    def send_rows(j, carry):
        @pl.when(row_target(j) != walk)
        def _():
            row_copy(j).start()

        @pl.when(row_target(j) == walk)
        def _():
            pltpu.make_async_copy(red.at[j], oper.at[walk], row_recv).start()

        return carry

    lax.fori_loop(0, 8, send_rows, 0)
    x_copy(2).start()
    for i in (1, 3):
        x_copy(i).wait_recv()
        sib_copy(i).start()

    @pl.when(computes)
    def _():
        pltpu.make_async_copy(oper, oper, row_recv).wait()
        walker = walker_ref[...]
        term = walker
        summed = walker.astype(jnp.float32)
        operator = oper[...].reshape(ORB, ORB)
        for degree in range(1, TERMS + 1):
            applied = jnp.dot(operator, term, preferred_element_type=jnp.float32)
            term = (applied / degree).astype(jnp.bfloat16)
            summed = summed + term.astype(jnp.float32)
        prop[...] = summed
        corr[...] = lax.dot_general(
            walker.astype(jnp.float32), summed, (((0,), (0,)), ((), ())), precision=HIGHEST,
            preferred_element_type=jnp.float32,
        )
        invert(corr)
        duals[y, z // 8] = jnp.dot(
            prop[...], corr[...], precision=HIGHEST, preferred_element_type=jnp.float32
        ).astype(jnp.bfloat16).reshape(2, 256, OCC)

    def hop(which, half, kind):
        block = duals.at[y, which, half]
        return remote(
            block, block, z_send.at[which, half, kind], z_recv.at[which, half],
            at((z + (6, 10, 3, 13, 2, 14, 1, 15)[kind]) % 16, y),
        )

    def away(which):
        return (z + 16 - which * 8 - chol) % 16

    def any_of(value, options):
        found = value == options[0]
        for option in options[1:]:
            found = jnp.logical_or(found, value == option)
        return found

    def relays(which):
        d = away(which)
        hub = any_of(d, (3, 13, 6, 10))
        return (
            (4, jnp.logical_and(d == 6, core == 0)),
            (5, jnp.logical_and(d == 10, core == 1)),
            (6, hub),
            (7, hub),
        )

    def y_copy(which, half, i):
        block = duals.at[y, which, half]
        return remote(
            block, block, y_send.at[which, half, i - 1], y_recv.at[which, half, i - 1],
            at(z, (y + i) % 4),
        )

    step = 1 + 2 * core

    def y_relay(which, half):
        block = duals.at[(y + 4 - step) % 4, which, half]
        return remote(
            block, block, y_send.at[which, half, 1], y_recv.at[which, half, 1],
            at(z, (y + step) % 4),
        )

    def settle(which, half):
        block = duals.at[y, which, half]

        @pl.when(away(which) != 0)
        def _():
            pltpu.make_async_copy(block, block, z_recv.at[which, half]).wait()

        for kind, condition in relays(which):

            @pl.when(condition)
            def _():
                hop(which, half, kind).start()

        y_copy(which, half, 1).start()
        y_copy(which, half, 3).start()

    def pass_on(which, half):
        block = duals.at[(y + 4 - step) % 4, which, half]
        pltpu.make_async_copy(block, block, y_recv.at[which, half, step - 1]).wait()
        y_relay(which, half).start()

    @pl.when(computes)
    def _():
        for kinds in ((0, 1), (2, 3), (6, 7)):
            for half in (0, 1):
                for kind in kinds:
                    hop(z // 8, half, kind).start()

    first = jnp.where(any_of(away(0), (0, 1, 15, 3, 13, 6, 10)), 0, 1)
    for which in (first, 1 - first):
        for half in (0, 1):
            settle(which, half)
    pass_on(first, 0)
    pass_on(first, 1)
    x_copy(2).wait_recv()
    sib_copy(2).start()
    pass_on(1 - first, 0)
    pass_on(1 - first, 1)

    def prop_copy(i):
        return remote(prop, prop_out, prop_send.at[i - 1], prop_recv, to((chol + i) % 8, walk))

    @pl.when(computes)
    def _():
        for i in range(1, 8):
            prop_copy(i).start()
        pltpu.make_async_copy(prop, prop_out, prop_recv).start()

    for i in range(4):
        sib_copy(i).wait_recv()

    def pair_energy(yy):
        block = jnp.concatenate(
            [duals[yy, which].reshape(ORB, OCC) for which in (0, 1)], axis=1
        )

        def vectors(i, sums):
            rows = rall[i].reshape(1024, ORB)
            products = jnp.dot(rows, block, preferred_element_type=jnp.float32)
            sums = list(sums)
            for g in range(8):
                for w in range(2):
                    one = products[g * 128 : g * 128 + 128, w * 128 : w * 128 + 128]
                    swapped = jnp.transpose(one.astype(jnp.bfloat16)).astype(jnp.float32)
                    terms = (one * swapped).reshape(16, 8, 128)
                    sums[w] = sums[w] + jnp.sum(terms, axis=0)
            return tuple(sums)

        zero = jnp.zeros((8, 128), jnp.float32)
        sums = lax.fori_loop(0, 4, vectors, (zero, zero))
        for which in (0, 1):
            pieces[yy, which] = jnp.sum(sums[which], axis=0, keepdims=True)

    def send_piece(yy, which):
        target = (which * 8 + 2 * x + yy // 2) * 4 + (yy % 2) * 2 + core
        piece = pieces.at[yy, which]
        place = collected.at[z * 4 + y]

        def send_to(peer, carry):
            same = jnp.logical_and(target == walk, peer == chol)

            @pl.when(jnp.logical_not(same))
            def _():
                remote(piece, place, piece_send, piece_recv, to(peer, target)).start()

            @pl.when(same)
            def _():
                pltpu.make_async_copy(piece, place, piece_recv).start()

            return carry

        lax.fori_loop(0, 8, send_to, 0)

    def each_pair(n, carry):
        i = jnp.where(n == 2, 3, jnp.where(n == 3, 2, n))
        yy = (y + 4 - i) % 4

        @pl.when(jnp.logical_and(n > 0, i != step))
        def _():
            for which in (0, 1):
                for half in (0, 1):
                    block = duals.at[yy, which, half]
                    pltpu.make_async_copy(block, block, y_recv.at[which, half, i - 1]).wait()

        pair_energy(yy)
        for which in (0, 1):
            send_piece(yy, which)
        return carry

    lax.fori_loop(0, 4, each_pair, 0)

    def drain_rows(j, carry):
        @pl.when(row_target(j) != walk)
        def _():
            row_copy(j).wait_send()

        return carry

    lax.fori_loop(0, 8, drain_rows, 0)
    sent = gathered.at[pl.ds(0, 63)]
    pltpu.make_async_copy(sent, sent, draw_send).wait()
    for n in range(2):
        for i in range(1, 8):
            part_copy(n, i).wait_send()
    for i in (1, 2, 3):
        x_copy(i).wait_send()
    for i in range(4):
        sib_copy(i).wait_send()
    for which in (0, 1):
        for half in (0, 1):
            for kind, condition in relays(which):

                @pl.when(condition)
                def _():
                    hop(which, half, kind).wait_send()

            y_copy(which, half, 1).wait_send()
            y_copy(which, half, 3).wait_send()
            y_relay(which, half).wait_send()

    @pl.when(computes)
    def _():
        for half in (0, 1):
            for kind in (0, 1, 2, 3, 6, 7):
                hop(z // 8, half, kind).wait_send()
        for i in range(1, 8):
            prop_copy(i).wait_send()

    def pieces_sent(count):
        gone = collected.at[pl.ds(0, count)]
        pltpu.make_async_copy(gone, gone, piece_send).wait()

    @pl.when(x_from == x)
    def _():
        pieces_sent(63)

    @pl.when(x_from != x)
    def _():
        pieces_sent(64)

    pltpu.make_async_copy(prop_out, prop_out, prop_recv).wait()
    pltpu.make_async_copy(collected, collected, piece_recv).wait()
    lanes = jnp.sum(collected[...].reshape(64, OCC), axis=0, keepdims=True)
    energy_out[...] = jnp.broadcast_to(-0.5 * jnp.sum(lanes, axis=1, keepdims=True), (8, 128))


def finish_kernel(prop_ref, energy_ref, prop_out, energy_out):
    prop_out[...] = prop_ref[...]
    energy_out[0] = energy_ref[0, 0]


def per_device(field_draws, chol_vectors, rotated_vectors, walkers):
    any_ref = pl.BlockSpec(memory_space=pl.ANY)
    vmem = pl.BlockSpec(memory_space=VMEM)
    propagated, exchange = pl.pallas_call(
        step_kernel,
        out_shape=(
            jax.ShapeDtypeStruct((ORB, OCC), jnp.float32),
            jax.ShapeDtypeStruct((8, 128), jnp.float32),
        ),
        in_specs=[vmem, any_ref, any_ref, vmem],
        out_specs=(vmem, vmem),
        scratch_shapes=[
            VMEM((2048, ORB), jnp.bfloat16),
            VMEM((1, 256), jnp.float32),
            VMEM((SLABS, 1, 256), jnp.float32),
            VMEM((512, 2048), jnp.bfloat16),
            VMEM((2, 512, 256), jnp.float32),
            VMEM((2, CHOL, 64, 256), jnp.bfloat16),
            VMEM((2, CHOL - 1, 64, 256), jnp.bfloat16),
            VMEM((8, 8, ORB), jnp.bfloat16),
            VMEM((SLABS, 8, ORB), jnp.bfloat16),
            VMEM((4, 2, 512, ORB), jnp.bfloat16),
            VMEM((ORB, OCC), jnp.float32),
            VMEM((OCC, OCC), jnp.float32),
            VMEM((4, 2, 2, 256, OCC), jnp.bfloat16),
            VMEM((4, 2, 1, 128), jnp.float32),
            VMEM((64, 1, 128), jnp.float32),
            DMA, DMA, DMA, DMA, DMA((2, 7)), DMA((2, 7)),
            DMA((8,)), DMA, DMA((3,)), DMA((3,)), DMA((4,)), DMA((4,)),
            DMA((2, 2, 8)), DMA((2, 2)), DMA((2, 2, 3)), DMA((2, 2, 3)), DMA((7,)), DMA,
            DMA, DMA,
        ],
        compiler_params=pltpu.CompilerParams(collective_id=0, has_side_effects=True),
        name="step",
    )(
        field_draws,
        chol_vectors.reshape(256 * 8, ORB),
        rotated_vectors.reshape(512, ORB),
        walkers.reshape(ORB, OCC),
    )
    propagated, exchange = pl.pallas_call(
        finish_kernel,
        out_shape=(
            jax.ShapeDtypeStruct((ORB, OCC), jnp.float32),
            jax.ShapeDtypeStruct((1,), jnp.float32),
        ),
        in_specs=[vmem, vmem],
        out_specs=(vmem, pl.BlockSpec(memory_space=pltpu.SMEM)),
        name="finish",
    )(propagated, exchange)
    return (propagated.reshape(1, ORB, OCC), exchange)


def solution(mesh):
    return jax.shard_map(
        per_device,
        mesh=mesh,
        in_specs=(
            P("walk", "chol"),
            P("chol", "walk", None),
            P(("chol", "walk"), None, None),
            P("walk", None, None),
        ),
        out_specs=(P("walk", None, None), P("walk")),
        check_vma=False,
    )
```
